32 devices in a mesh: band: 8 (over z, x), dom: 4 (over y, core).
Axes of the slice: x: 2, y: 2, z: 4, core: 2. Of those that a mesh axis runs over, the one named last changes fastest.
Arguments:
- orbitals: bfloat16 [512, 16, 2048], P('band', 'dom'), may hold values from -6 to 6
- potential: float32 [16, 2048], P('dom'), may hold values from 0 to 2
- bounds: float32 [2], replicated, may hold values from 1 to 10, as said below
Outputs:
- rotated: bfloat16 [512, 16, 2048], P('band', 'dom')
- projected: float32 [512, 512], replicated
The draws below stay inside these ranges and needn't reach their ends.
Inputs may be any that keep to these rules, and one draw needn't show every extreme that they name: bounds[0] lies in 1 to 2 and bounds[1] in 8.5 to 10, above the whole spectrum of H.
All inputs are finite; a program needn't handle non-finite values.
Results may differ from the reference program's by a relative error of at most 0.006.
Values may be sent and summed in bfloat16 or wider, within the bound.
A program may use at most 128 MiB of HBM per device.

```python
import math
import jax
import jax.numpy as jnp
from jax import lax

BANDS = 512
GRID_Y = 64
GRID_Z = 32
DEG = 8
NS_STEPS = 8
GRID_X = 16
GRID_YZ = 2048


def draw_bounds(key, part):
    first_key, second_key = jax.random.split(jax.random.fold_in(key, 17))
    lower_cut = jax.random.uniform(first_key, (), jnp.float32, 1.0, 2.0)
    upper_cut = jax.random.uniform(second_key, (), jnp.float32, 8.5, 10.0)
    return jnp.stack([lower_cut, upper_cut]).astype(jnp.float32)


def block_scale(rng, extent, pieces, smallest, largest):
    factor_of = 1.0
    for dim, parts in pieces:
        steps = jax.random.uniform(jax.random.fold_in(jax.random.fold_in(rng, 6), dim), (parts,), jnp.float32, smallest / len(pieces), largest / len(pieces))
        factor_of = factor_of * jnp.repeat(jnp.exp(steps), extent[dim] // parts).reshape((-1,) + (1,) * (len(extent) - 1 - dim))
    return factor_of


def centred(key, dims, width, bound, pieces=(), kind=jnp.bfloat16):
    entries = jax.random.normal(key, dims, jnp.float32) * width
    if len(pieces) > 0:
        entries = block_scale(key, dims, pieces, -0.22, 0.18) * entries
    return jnp.clip(entries, min=-bound, max=bound).astype(kind)


def setup_inputs(seed: int = 0) -> dict:
    key_of = jax.random.split(jax.random.key(seed), 4)
    orbitals = centred(key_of[0], (BANDS, GRID_X, GRID_YZ), 1.0, 6.0, ((0, 8), (1, 4)))
    potential = jnp.clip(2.0 * jax.random.uniform(key_of[1], (GRID_X, GRID_YZ), jnp.float32) ** block_scale(key_of[1], (GRID_X, GRID_YZ), ((0, 4),), -0.2, 0.2), 0.0, 2.0)
    bounds = draw_bounds(jax.random.fold_in(key_of[3], 71), 0)
    return dict(orbitals=orbitals, potential=potential, bounds=bounds)


def hamiltonian(field, pot_grid):
    beside = jnp.roll(field, -1, 1) + jnp.roll(field, 1, 1)
    beside = beside + jnp.roll(field, -1, 2) + jnp.roll(field, 1, 2)
    beside = beside + jnp.roll(field, -1, 3) + jnp.roll(field, 1, 3)
    return -0.5 * (beside - 6.0 * field) + pot_grid * field

def filter_group(orbital_block, pot_grid, lower_cut, upper_cut):
    half_width = (upper_cut - lower_cut) / 2.0
    centre = (upper_cut + lower_cut) / 2.0
    start = orbital_block.astype(jnp.float32)
    earlier = start
    current = (hamiltonian(start, pot_grid) - centre * start) / half_width
    for repeat in range(DEG - 1):
        following = 2.0 * (hamiltonian(current, pot_grid) - centre * current) / half_width - earlier
        earlier = current
        current = following
    applied = hamiltonian(current, pot_grid)
    return (current.astype(jnp.bfloat16), applied.astype(jnp.bfloat16))

def reference(orbitals, potential, bounds):
    grid_x = orbitals.shape[1]
    group_size = math.gcd(BANDS, 64)
    pot_grid = potential.reshape(grid_x, GRID_Y, GRID_Z)
    blocks = orbitals.reshape(BANDS // group_size, group_size, grid_x, GRID_Y, GRID_Z)
    lower_cut = bounds[0]
    upper_cut = bounds[1]
    filt, applied = lax.map(lambda item: filter_group(item, pot_grid, lower_cut, upper_cut), blocks)
    points = grid_x * GRID_Y * GRID_Z
    filt = filt.reshape(BANDS, points)
    applied = applied.reshape(BANDS, points)
    cell_volume = 1.0 / points
    correlation = jnp.dot(filt, filt.T, preferred_element_type=jnp.float32) * cell_volume
    hamil_sub = jnp.dot(filt, applied.T, preferred_element_type=jnp.float32) * cell_volume
    scale = jnp.sqrt(jnp.sum(correlation * correlation) + 1e-06)
    scaled = correlation / scale
    identity = jnp.eye(BANDS, dtype=jnp.float32)
    inverse = identity
    high = lax.Precision.HIGHEST
    for repeat in range(NS_STEPS):
        factor = 1.5 * identity - 0.5 * jnp.dot(inverse, scaled, precision=high)
        scaled = jnp.dot(factor, scaled, precision=high)
        inverse = jnp.dot(factor, inverse, precision=high)
    transform = inverse / jnp.sqrt(scale)
    projected = jnp.dot(jnp.dot(transform.T, hamil_sub, precision=high), transform, precision=high)
    rotated = jnp.dot(transform.T, filt.astype(jnp.float32), precision=high).astype(jnp.bfloat16)
    return (rotated.reshape(BANDS, grid_x, GRID_Y * GRID_Z), projected)
```

```python
import functools

import jax
import jax.numpy as jnp
from jax import lax
from jax.experimental import pallas as pl
from jax.experimental.pallas import tpu as pltpu
from jax.sharding import PartitionSpec as P

GRID_Z = 32
DEG = 8
NS_STEPS = 8
LANES = 128


def filter_kernel(scal_ref, cells_ref, pot_ref, filt_ref, applied_ref, field, coef):
    planes, bands, width = cells_ref.shape
    blocks_per_plane = filt_ref.shape[0] // planes
    block = filt_ref.shape[2]
    rows = min(8, bands)
    chunks = width // LANES
    inv_half = scal_ref[0]
    centre = scal_ref[1]
    lane = lax.broadcasted_iota(jnp.int32, (rows, LANES), 1)
    z_cell = lane % GRID_Z
    z_last = z_cell == GRID_Z - 1
    z_first = z_cell == 0
    y_last = lane >= LANES - GRID_Z
    y_first = lane < GRID_Z

    def load(slot, x, start):
        return [
            field[slot, x, pl.ds(start, rows), pl.ds(c * LANES, LANES)] for c in range(chunks)
        ]

    def update(slot, x, start, weight, emit):
        before = lax.rem(x + planes - 1, planes)
        after = lax.rem(x + 1, planes)
        mine = load(slot, x, start)
        ups = [pltpu.roll(v, LANES - GRID_Z, 1) for v in mine]
        downs = [pltpu.roll(v, GRID_Z, 1) for v in mine]
        for c in range(chunks):
            v = mine[c]
            cols = pl.ds(c * LANES, LANES)
            total = field[slot, after, pl.ds(start, rows), cols]
            total = total + field[slot, before, pl.ds(start, rows), cols]
            total = total + jnp.where(y_last, ups[(c + 1) % chunks], ups[c])
            total = total + jnp.where(y_first, downs[(c - 1) % chunks], downs[c])
            total = total + jnp.where(
                z_last, pltpu.roll(v, GRID_Z - 1, 1), pltpu.roll(v, LANES - 1, 1)
            )
            total = total + jnp.where(
                z_first, pltpu.roll(v, LANES - GRID_Z + 1, 1), pltpu.roll(v, 1, 1)
            )
            emit(c, cols, v, weight * total)

    def sweep(step):
        def run(x, carry):
            for start in range(0, bands, rows):
                step(x, start)
            return carry

        lax.fori_loop(0, planes, run, 0)

    def setup(x, carry):
        field[0, x] = cells_ref[x].astype(jnp.float32)
        coef[x] = (3.0 + pot_ref[x] - centre) * (2.0 * inv_half)
        return carry

    lax.fori_loop(0, planes, setup, 0)

    def first(x, start):
        def emit(c, cols, v, part):
            field[1, x, pl.ds(start, rows), cols] = part + (0.5 * coef[x, :, cols]) * v

        update(0, x, start, -0.5 * inv_half, emit)

    sweep(first)

    def middle(k, carry):
        slot = lax.rem(k, 2)
        other = 1 - slot

        def step(x, start):
            def emit(c, cols, v, part):
                where = (other, x, pl.ds(start, rows), cols)
                field[where] = part + coef[x, :, cols] * v - field[where]

            update(slot, x, start, -inv_half, emit)

        sweep(step)
        return carry

    lax.fori_loop(1, DEG, middle, 0)
    last_slot = DEG % 2

    def last(x, carry):
        for start in range(0, bands, rows):

            def emit(c, cols, v, part):
                piece = (c * LANES) // block
                inner = (c * LANES) % block
                where = (
                    x * blocks_per_plane + piece,
                    pl.ds(start, rows),
                    pl.ds(inner, LANES),
                )
                filt_ref[where] = v.astype(jnp.bfloat16)
                applied_ref[where] = (part + (3.0 + pot_ref[x, :, cols]) * v).astype(jnp.bfloat16)

            update(last_slot, x, start, -0.5, emit)
        return carry

    lax.fori_loop(0, planes, last, 0)


def filter_bands(cells, potential, scalars, devices):
    planes, bands, width = cells.shape
    block = planes * width // devices
    out = jax.ShapeDtypeStruct((devices, bands, block), jnp.bfloat16)
    vmem = pl.BlockSpec(memory_space=pltpu.VMEM)
    return pl.pallas_call(
        filter_kernel,
        out_shape=(out, out),
        in_specs=[pl.BlockSpec(memory_space=pltpu.SMEM), vmem, vmem],
        out_specs=(vmem, vmem),
        scratch_shapes=[
            pltpu.VMEM((2, planes, bands, width), jnp.float32),
            pltpu.VMEM((planes, 1, width), jnp.float32),
        ],
        compiler_params=pltpu.CompilerParams(vmem_limit_bytes=32 << 20),
    )(scalars, cells, potential)


def split(value):
    high = value.astype(jnp.bfloat16)
    return high, (value - high.astype(jnp.float32)).astype(jnp.bfloat16)


def dot(a, b):
    return jnp.dot(a, b, preferred_element_type=jnp.float32)


def dot3(a, b):
    (a_high, a_low), (b_high, b_low) = a, b
    return dot(a_high, b_high) + (dot(a_high, b_low) + dot(a_low, b_high))


def rotate_kernel(groups, corr_ref, hamil_ref, filt_ref, out_ref, proj_ref, y_ref, z_ref, t_ref):
    size = corr_ref.shape[0]
    outer, inner, width = groups
    row = lax.broadcasted_iota(jnp.int32, (size, size), 0)
    col = lax.broadcasted_iota(jnp.int32, (size, size), 1)
    diag = jnp.where(row == col, 1.5, 0.0)
    corr = corr_ref[...]
    scale = jnp.sqrt(jnp.sum(corr * corr) + 1e-06)
    scaled = corr / scale
    factor = diag - 0.5 * scaled
    z_ref[...] = factor
    y_ref[...] = dot3(split(factor), split(scaled))

    def step(k, carry):
        y = split(y_ref[...])
        z = split(z_ref[...])
        factor = split(diag - 0.5 * dot3(z, y))
        y_ref[...] = dot3(factor, y)
        z_ref[...] = dot3(factor, z)
        return carry

    lax.fori_loop(1, NS_STEPS - 1, step, 0)
    y = split(y_ref[...])
    z = split(z_ref[...])
    factor = split(diag - 0.5 * dot3(z, y))
    t_ref[...] = dot3(factor, z) / jnp.sqrt(scale)
    for i in range(outer):
        for j in range(inner):
            z_ref[pl.ds((j * outer + i) * width, width), :] = t_ref[
                pl.ds((i * inner + j) * width, width), :
            ]
    trans = split(z_ref[...])
    half = split(dot3(trans, split(hamil_ref[...])))
    contract = (((1,), (1,)), ((), ()))

    def dot_t(a, b):
        return lax.dot_general(a, b, contract, preferred_element_type=jnp.float32)

    proj_ref[...] = dot_t(half[0], trans[0]) + (
        dot_t(half[0], trans[1]) + dot_t(half[1], trans[0])
    )
    filt = filt_ref[...]
    out_ref[...] = (dot(trans[0], filt) + dot(trans[1], filt)).astype(jnp.bfloat16)


def rotate(corr, hamil, filt, groups):
    size = corr.shape[0]
    vmem = pl.BlockSpec(memory_space=pltpu.VMEM)
    square = pltpu.VMEM((size, size), jnp.float32)
    return pl.pallas_call(
        functools.partial(rotate_kernel, groups),
        out_shape=(
            jax.ShapeDtypeStruct(filt.shape, jnp.bfloat16),
            jax.ShapeDtypeStruct(corr.shape, jnp.float32),
        ),
        in_specs=[vmem] * 3,
        out_specs=(vmem, vmem),
        scratch_shapes=[square] * 3,
        compiler_params=pltpu.CompilerParams(vmem_limit_bytes=40 << 20),
    )(corr, hamil, filt)


def body(orbitals, potential, bounds):
    bands, slab, width = orbitals.shape
    doms = lax.axis_size("dom")
    groups = lax.axis_size("band")
    devices = doms * groups
    total_bands = bands * groups
    mine = bands // doms
    everyone = ("dom", "band")
    half_width = (bounds[1] - bounds[0]) / 2.0
    centre = (bounds[1] + bounds[0]) / 2.0
    cell_volume = 1.0 / (slab * doms * width)

    sent = orbitals.reshape(doms, mine, slab, width).transpose(0, 2, 1, 3)
    cells = lax.all_to_all(sent, "dom", split_axis=0, concat_axis=0, tiled=True)
    cells = cells.reshape(doms * slab, mine, width)
    pot = lax.all_to_all(
        jnp.broadcast_to(potential, (doms, slab, width)), "dom", split_axis=0, concat_axis=0, tiled=True
    ).reshape(doms * slab, 1, width)
    filt, applied = filter_bands(cells, pot, jnp.stack([1.0 / half_width, centre]), devices)
    filt = lax.all_to_all(filt, everyone, split_axis=0, concat_axis=0, tiled=True)
    applied = lax.all_to_all(applied, everyone, split_axis=0, concat_axis=0, tiled=True)
    filt = filt.reshape(total_bands, -1)
    applied = applied.reshape(total_bands, -1)
    contract = (((1,), (1,)), ((), ()))

    def summed(other):
        part = lax.dot_general(filt, other, contract, preferred_element_type=jnp.float32)
        part = part.astype(jnp.bfloat16).reshape(devices, total_bands // devices, total_bands)
        part = lax.all_to_all(part, everyone, split_axis=0, concat_axis=0, tiled=True)
        return jnp.sum(part.astype(jnp.float32), axis=0) * cell_volume

    corr = lax.all_gather(summed(filt), everyone, axis=0, tiled=True)
    hamil = lax.all_gather(summed(applied), everyone, axis=0, tiled=True)
    rotated, projected = rotate(corr, hamil, filt, (doms, groups, mine))
    out = lax.all_to_all(rotated, "band", split_axis=0, concat_axis=1, tiled=True)
    return out.reshape(bands, slab, width), projected


def solution(mesh):
    return jax.shard_map(
        body,
        mesh=mesh,
        in_specs=(P("band", "dom", None), P("dom", None), P()),
        out_specs=(P("band", "dom", None), P()),
        check_vma=False,
    )
```

```python
import functools

import jax
import jax.numpy as jnp
from jax import lax
from jax.experimental import pallas as pl
from jax.experimental.pallas import tpu as pltpu
from jax.sharding import PartitionSpec as P

GRID_Z = 32
DEG = 8
NS_STEPS = 8
LANES = 128
TILE_ROWS = 16


def filter_kernel(scal_ref, cells_ref, pot_ref, sums_ref, filt_ref, applied_ref, field, high, low, coef):
    planes, bands, width = cells_ref.shape
    rows = planes * bands
    blocks_per_plane = filt_ref.shape[0] // planes
    block = filt_ref.shape[2]
    tile = sums_ref.shape[1]
    inv_half = scal_ref[0]
    centre = scal_ref[1]

    for x in range(planes):
        mine = pl.ds(x * bands, bands)
        coef[mine, :] = jnp.broadcast_to(3.0 + pot_ref[x], (bands, width))
        start = cells_ref[x].astype(jnp.float32)
        field[0, mine, :] = start
    for c in range(width // tile):
        cols = pl.ds(c * tile, tile)
        start = field[0, :, cols]
        high[0, :, cols] = start.astype(jnp.bfloat16)
        low[0, :, cols] = jnp.zeros((rows, tile), jnp.bfloat16)

    def shifted(v, by):
        if bands % 8 == 0:
            return jnp.concatenate([v[by:], v[:by]], axis=0)
        return pltpu.roll(v, (rows - by) % rows, 0)

    def neighbours(slot, c, v):
        cols = pl.ds(pl.multiple_of(c * tile, tile), tile)
        left = pl.ds(pl.multiple_of(lax.rem(c * tile + width - LANES, width), LANES), LANES)
        right = pl.ds(pl.multiple_of(lax.rem(c * tile + tile, width), LANES), LANES)

        def part(ref):
            wide = jnp.concatenate([ref[slot, :, left], ref[slot, :, cols], ref[slot, :, right]], axis=1)
            return dot(wide, sums_ref[...])

        return part(high) + part(low) + (shifted(v, bands) + shifted(v, rows - bands))

    def sweep(slot, other, weight, diagonal, first):
        def run(c, carry):
            cols = pl.ds(pl.multiple_of(c * tile, tile), tile)
            v = field[slot, :, cols]
            fresh = weight * neighbours(slot, c, v) + (coef[:, cols] * diagonal[0] + diagonal[1]) * v
            if not first:
                fresh = fresh - field[other, :, cols]
            field[other, :, cols] = fresh
            top, rest = split(fresh)
            high[other, :, cols] = top
            low[other, :, cols] = rest
            return carry

        lax.fori_loop(0, width // tile, run, 0)

    sweep(0, 1, -0.5 * inv_half, (inv_half, -centre * inv_half), True)

    def middle(k, carry):
        slot = lax.rem(k, 2)
        sweep(slot, 1 - slot, -inv_half, (2.0 * inv_half, -2.0 * centre * inv_half), False)
        return carry

    lax.fori_loop(1, DEG, middle, 0)
    slot = DEG % 2
    for c in range(width // tile):
        cols = pl.ds(c * tile, tile)
        v = field[slot, :, cols]
        applied = coef[:, cols] * v - 0.5 * neighbours(slot, c, v)
        piece, inner = divmod(c * tile, block)
        for x in range(planes):
            where = (x * blocks_per_plane + piece, slice(None), pl.ds(inner, tile))
            filt_ref[where] = v[x * bands : (x + 1) * bands].astype(jnp.bfloat16)
            applied_ref[where] = applied[x * bands : (x + 1) * bands].astype(jnp.bfloat16)


def neighbour_sums(tile):
    source = lax.broadcasted_iota(jnp.int32, (tile + 2 * LANES, tile), 0) - LANES
    target = lax.broadcasted_iota(jnp.int32, (tile + 2 * LANES, tile), 1)
    step = source - target
    same_row = (source >= 0) & (source // GRID_Z == target // GRID_Z)
    apart = lax.rem(step + GRID_Z, GRID_Z)
    beside_z = same_row & ((apart == 1) | (apart == GRID_Z - 1))
    beside_y = (step == GRID_Z) | (step == -GRID_Z)
    return (beside_z | beside_y).astype(jnp.bfloat16)


def filter_bands(cells, potential, scalars, devices):
    planes, bands, width = cells.shape
    rows = planes * bands
    block = planes * width // devices
    out = jax.ShapeDtypeStruct((devices, bands, block), jnp.bfloat16)
    vmem = pl.BlockSpec(memory_space=pltpu.VMEM)
    return pl.pallas_call(
        filter_kernel,
        out_shape=(out, out),
        in_specs=[pl.BlockSpec(memory_space=pltpu.SMEM), vmem, vmem, vmem],
        out_specs=(vmem, vmem),
        scratch_shapes=[
            pltpu.VMEM((2, rows, width), jnp.float32),
            pltpu.VMEM((2, rows, width), jnp.bfloat16),
            pltpu.VMEM((2, rows, width), jnp.bfloat16),
            pltpu.VMEM((rows, width), jnp.float32),
        ],
        compiler_params=pltpu.CompilerParams(vmem_limit_bytes=48 << 20),
    )(scalars, cells, potential, neighbour_sums(min(256, block)))


def split(value):
    spread = value * 65537.0
    high = spread - (spread - value)
    return high.astype(jnp.bfloat16), (value - high).astype(jnp.bfloat16)


def dot(a, b):
    return jnp.dot(a, b, preferred_element_type=jnp.float32)


def dot3(a, b):
    (a_high, a_low), (b_high, b_low) = a, b
    return dot(a_high, b_high) + (dot(a_high, b_low) + dot(a_low, b_high))


def exchange_bits(doms, groups):
    dom = [("dom", 1 << i) for i in range(1, (doms - 1).bit_length())]
    band = [("band", 1 << i) for i in range((groups - 1).bit_length())]
    core = [("dom", 1)]
    return core + band[:1] + dom + band[1:], core + dom + band


def reduce_kernel(
    bits, cell_volume, groups,
    filt_ref, applied_ref, out_ref, proj_ref,
    total, send, recv, gath, y_ref, z_ref, t_ref, send_sem, recv_sem,
):
    size = filt_ref.shape[0]
    index = {axis: lax.axis_index(axis) for axis in ("dom", "band")}

    def partner(axis, bit):
        mine = lax.rem(index[axis] // bit, 2)
        return mine, {axis: index[axis] + bit - 2 * bit * mine}

    barrier = pltpu.get_barrier_semaphore()
    for axis, bit in bits[0]:
        pl.semaphore_signal(
            barrier, inc=1, device_id=partner(axis, bit)[1], device_id_type=pl.DeviceIdType.MESH
        )

    pairs = (((1,), (1,)), ((), ()))
    for stream, other in enumerate((filt_ref, applied_ref)):
        for lead in range(0, size, 256):
            total[stream, pl.ds(lead, 256), :] = cell_volume * lax.dot_general(
                filt_ref[pl.ds(lead, 256), :], other[...], pairs, preferred_element_type=jnp.float32
            )
    pl.semaphore_wait(barrier, len(bits[0]))

    def copy(stream, number, source, target, device):
        made = pltpu.make_async_remote_copy(
            src_ref=source,
            dst_ref=target,
            send_sem=send_sem.at[stream, number],
            recv_sem=recv_sem.at[stream, number],
            device_id=device,
            device_id_type=pl.DeviceIdType.MESH,
        )
        made.start()
        return made

    stages = len(bits[0])
    start = [jnp.int32(0)] * 2
    halved = [[], []]
    length, offset = size, 0
    for stage in range(stages):
        halve = length >= 2 * TILE_ROWS
        count = length // 2 if halve else length
        space = pl.ds(offset, count)
        flight = []
        for stream in range(2):
            axis, bit = bits[stream][stage]
            mine, device = partner(axis, bit)
            give = start[stream] + (1 - mine) * count if halve else start[stream]
            keep = start[stream] + mine * count if halve else start[stream]
            give = pl.multiple_of(give, TILE_ROWS)
            send[stream, space, :] = total[stream, pl.ds(give, count), :]
            flight.append(
                copy(stream, stage, send.at[stream, space], recv.at[stream, space], device)
            )
            start[stream] = pl.multiple_of(keep, TILE_ROWS)
            if halve:
                halved[stream].append((stage, mine, device))
        for stream in range(2):
            flight[stream].wait()
            kept = pl.ds(start[stream], count)
            if halve:
                own = total[stream, kept, :]
            else:
                own = send[stream, space, :]
            total[stream, kept, :] = own + recv[stream, space, :]
        length = count
        offset += count

    for stream in range(2):
        kept = pl.ds(start[stream], length)
        gath[stream, kept, :] = total[stream, kept, :]
    for back in range(len(halved[0]) - 1, -1, -1):
        flight = []
        for stream in range(2):
            stage, mine, device = halved[stream][back]
            area = gath.at[stream, pl.ds(start[stream], length)]
            flight.append(copy(stream, stages + stage, area, area, device))
            start[stream] = pl.multiple_of(start[stream] - mine * length, TILE_ROWS)
        for made in flight:
            made.wait()
        length *= 2

    outer, inner, width = groups
    row = lax.broadcasted_iota(jnp.int32, (size, size), 0)
    col = lax.broadcasted_iota(jnp.int32, (size, size), 1)
    diag = jnp.where(row == col, 1.5, 0.0)
    corr = gath[0]
    scale = jnp.sqrt(jnp.sum(corr * corr) + 1e-06)
    scaled = corr / scale
    factor = diag - 0.5 * scaled
    z_ref[...] = factor
    y_ref[...] = dot3(split(factor), split(scaled))

    def step(k, carry):
        y = split(y_ref[...])
        z = split(z_ref[...])
        factor = split(diag - 0.5 * dot3(z, y))
        y_ref[...] = dot3(factor, y)
        z_ref[...] = dot3(factor, z)
        return carry

    lax.fori_loop(1, NS_STEPS - 1, step, 0)
    y = split(y_ref[...])
    z = split(z_ref[...])
    factor = split(diag - 0.5 * dot3(z, y))
    t_ref[...] = dot3(factor, z) / jnp.sqrt(scale)
    for i in range(outer):
        for j in range(inner):
            z_ref[pl.ds((j * outer + i) * width, width), :] = t_ref[
                pl.ds((i * inner + j) * width, width), :
            ]
    trans = split(z_ref[...])
    half = split(dot3(trans, split(gath[1])))
    contract = (((1,), (1,)), ((), ()))

    def dot_t(a, b):
        return lax.dot_general(a, b, contract, preferred_element_type=jnp.float32)

    proj_ref[...] = dot_t(half[0], trans[0]) + (
        dot_t(half[0], trans[1]) + dot_t(half[1], trans[0])
    )
    filt = filt_ref[...]
    out_ref[...] = (dot(trans[0], filt) + dot(trans[1], filt)).astype(jnp.bfloat16)


def rotate(filt, applied, cell_volume, groups):
    size = filt.shape[0]
    bits = exchange_bits(groups[0], groups[1])
    vmem = pl.BlockSpec(memory_space=pltpu.VMEM)
    square = pltpu.VMEM((size, size), jnp.float32)
    room = size + TILE_ROWS * len(bits[0])
    sems = pltpu.SemaphoreType.DMA((2, 2 * len(bits[0])))
    return pl.pallas_call(
        functools.partial(reduce_kernel, bits, cell_volume, groups),
        out_shape=(
            jax.ShapeDtypeStruct(filt.shape, jnp.bfloat16),
            jax.ShapeDtypeStruct((size, size), jnp.float32),
        ),
        in_specs=[vmem] * 2,
        out_specs=(vmem, vmem),
        scratch_shapes=[
            pltpu.VMEM((2, size, size), jnp.float32),
            pltpu.VMEM((2, room, size), jnp.float32),
            pltpu.VMEM((2, room, size), jnp.float32),
            pltpu.VMEM((2, size, size), jnp.float32),
            square,
            square,
            square,
            sems,
            sems,
        ],
        compiler_params=pltpu.CompilerParams(
            vmem_limit_bytes=56 << 20, collective_id=0, has_side_effects=True
        ),
    )(filt, applied)


def body(orbitals, potential, bounds):
    bands, slab, width = orbitals.shape
    doms = lax.axis_size("dom")
    groups = lax.axis_size("band")
    devices = doms * groups
    total_bands = bands * groups
    mine = bands // doms
    everyone = ("dom", "band")
    half_width = (bounds[1] - bounds[0]) / 2.0
    centre = (bounds[1] + bounds[0]) / 2.0
    cell_volume = 1.0 / (slab * doms * width)

    sent = orbitals.reshape(doms, mine, slab, width).transpose(0, 2, 1, 3)
    cells = lax.all_to_all(sent, "dom", split_axis=0, concat_axis=0, tiled=True)
    cells = cells.reshape(doms * slab, mine, width)
    pot = lax.all_to_all(
        jnp.broadcast_to(potential, (doms, slab, width)), "dom", split_axis=0, concat_axis=0, tiled=True
    ).reshape(doms * slab, 1, width)
    filt, applied = filter_bands(cells, pot, jnp.stack([1.0 / half_width, centre]), devices)
    filt = lax.all_to_all(filt, everyone, split_axis=0, concat_axis=0, tiled=True)
    applied = lax.all_to_all(applied, everyone, split_axis=0, concat_axis=0, tiled=True)
    filt = filt.reshape(total_bands, -1)
    applied = applied.reshape(total_bands, -1)
    rotated, projected = rotate(filt, applied, cell_volume, (doms, groups, mine))
    out = lax.all_to_all(rotated, "band", split_axis=0, concat_axis=1, tiled=True)
    return out.reshape(bands, slab, width), projected


def solution(mesh):
    return jax.shard_map(
        body,
        mesh=mesh,
        in_specs=(P("band", "dom", None), P("dom", None), P()),
        out_specs=(P("band", "dom", None), P()),
        check_vma=False,
    )
```
